32 devices in a mesh: slab: 16 (over z, x, core), vec: 2 (over y).
Axes of the slice: x: 2, y: 2, z: 4, core: 2. Of those that a mesh axis runs over, the one named last changes fastest.
Arguments:
- block: bfloat16 [64, 3, 16, 16, 128], P('vec', None, 'slab'), may hold values from -8 to 8
- labels: int32 [16, 16, 128], P('slab'), may hold values from 0 to 3
- flags: int32 [16, 16, 128], P('slab'), may hold values 0 or 1
- stiffness: float32 [4], replicated, may hold values from 0.25 to 2.5
- density: float32 [4], replicated, may hold values from 0.5 to 4
Outputs:
- filtered: bfloat16 [64, 3, 16, 16, 128], P('vec', None, 'slab')
- gram: float32 [64, 64], P('vec')
The draws below stay inside these ranges and needn't reach their ends.
Inputs may be any that keep to these rules, and one draw needn't show every extreme that they name: `labels`: 0 steel, 1 weld, 2 bearing, 3 void filler.
All inputs are finite; a program needn't handle non-finite values. No bound on the sum of `flags` on one device may be relied on, other than what follows from the above.
Results may differ from the reference program's by a relative error of at most 0.0049.
Values may be sent and summed in bfloat16 or wider, within the bound.
A program may use at most 64 MiB of HBM per device.

```python
import math
import jax
import jax.numpy as jnp
from jax import lax

NY = 16
NZ = 128
VEC_DEV = 32
MATERIALS = 4
VECS = 64
NA = 16
DOFS = 98304
N_VEC = 2


def draw_block(key, part):
    subkeys = jax.random.split(key, 5)
    shape = (VECS, 3, NA, NY, NZ)
    position = jnp.arange(NA, dtype=jnp.float32) / NA
    mixed = jnp.clip(jax.random.normal(subkeys[0], shape, jnp.float32), -4.0, 4.0)
    axial_ramp = 1.0 + 0.8 * position
    segments = max((VECS - 1).bit_length(), 1)
    magnitude = jax.random.uniform(subkeys[1], (segments, VECS), jnp.float32, 0.7, 1.0)
    signs = jnp.where(jax.random.bernoulli(subkeys[2], 0.5, (segments, VECS)), jnp.float32(1.0), jnp.float32(-1.0))
    own_weight = magnitude * signs
    cross_weight = jax.random.uniform(subkeys[3], (segments, VECS), jnp.float32, -0.7, 0.7)
    for segment in range(segments):
        partner = jnp.roll(mixed, -2 ** segment, axis=0)
        mixed = (own_weight[segment][:, None, None, None, None] * mixed + cross_weight[segment][:, None, None, None, None] * partner) * 1.058
    scales = jnp.exp(jax.random.uniform(subkeys[4], (VECS,), jnp.float32, 0.0, 1.1)) * 0.5
    summed = mixed * scales[:, None, None, None, None] * axial_ramp[None, None, :, None, None]
    return jnp.clip(summed, -8.0, 8.0).astype(jnp.bfloat16)


def touch_ends(array, key, least, high):
    index_at = [jax.random.randint(jax.random.fold_in(key, axis), (), 0, length) for axis, length in enumerate(array.shape)]
    main_axis = array.shape.index(max(array.shape))
    beside = index_at[:main_axis] + [(index_at[main_axis] + 1) % array.shape[main_axis]] + index_at[main_axis + 1:]
    return array.at[tuple(index_at)].set(least).at[tuple(beside)].set(high)


def setup_inputs(seed: int = 0) -> dict:
    key_of = jax.random.split(jax.random.key(seed), 6)
    return {
        "block": draw_block(jax.random.fold_in(key_of[5], 71), 0),
        "labels": touch_ends(jax.random.randint(key_of[1], (NA, NY, NZ), 0, MATERIALS), jax.random.fold_in(key_of[1], 1), 0, MATERIALS - 1).astype(jnp.int32),
        "flags": touch_ends((jax.random.randint(key_of[2], (NA, NY, NZ), 0, 8) < 1).astype(jnp.int32), jax.random.fold_in(key_of[2], 1), 0, 1),
        "stiffness": jnp.clip(jnp.exp(jax.random.uniform(key_of[3], (MATERIALS,), jnp.float32, math.log(0.25), math.log(2.5))), 0.25, 2.5),
        "density": jnp.clip(jnp.exp(jax.random.uniform(key_of[4], (MATERIALS,), jnp.float32, math.log(0.5), math.log(4.0))), 0.5, 4.0),
    }


axial_modulus = 0.75
shear_modulus = 0.25
dilation_modulus = 0.5

def lookup_table(table, labels):
    summed = jnp.zeros(labels.shape, jnp.float32)
    for material in range(table.shape[0]):
        summed = summed + jnp.where(labels == material, table[material], jnp.float32(0.0))
    return summed

def stencil_pass(values, axis_index, operation):
    length = values.shape[axis_index] - 2
    lower = lax.slice_in_dim(values, 0, length, axis=axis_index)
    middle = lax.slice_in_dim(values, 1, length + 1, axis=axis_index)
    higher = lax.slice_in_dim(values, 2, length + 2, axis=axis_index)
    if operation == 'avg':
        return (lower + 4.0 * middle + higher) / 6.0
    if operation == 'second':
        return lower - 2.0 * middle + higher
    return (higher - lower) * 0.5

def separable(values, operations):
    for position in range(3):
        values = stencil_pass(values, position + 1, operations[position])
    return values

def navier(padded):
    components = [padded[:, source] for source in range(3)]
    results = []
    for target in range(3):
        summed = 0.0
        for direction in range(3):
            operations = ['avg', 'avg', 'avg']
            operations[direction] = 'second'
            factor = axial_modulus if direction == target else shear_modulus
            summed = summed - factor * separable(components[target], operations)
        for source in range(3):
            if source != target:
                operations = ['avg', 'avg', 'avg']
                operations[target] = 'first'
                operations[source] = 'first'
                summed = summed - dilation_modulus * separable(components[source], operations)
        results.append(summed)
    return jnp.stack(results, axis=1)

def reference(block, labels, flags, stiffness, density):
    gain = jnp.sqrt(lookup_table(stiffness, labels)) * (1 - flags).astype(jnp.float32)
    mass = lookup_table(density, labels)
    groups = block.reshape(N_VEC, VEC_DEV, 3, NA, NY, NZ)

    def filter_group(piece):
        scaled = (gain * piece.astype(jnp.float32)).astype(jnp.bfloat16)
        scaled = lax.optimization_barrier(scaled).astype(jnp.float32)
        padded = jnp.pad(scaled, ((0, 0), (0, 0), (1, 1), (1, 1), (1, 1)))
        return (gain * navier(padded)).astype(jnp.bfloat16)
    filtered_groups = lax.map(filter_group, groups)

    def weigh_group(piece):
        return (mass * piece.astype(jnp.float32)).astype(jnp.bfloat16)
    weighted_groups = lax.map(weigh_group, filtered_groups)
    filtered = filtered_groups.reshape(VECS, 3, NA, NY, NZ)
    flat_left = filtered.reshape(VECS, DOFS)
    flat_right = weighted_groups.reshape(VECS, DOFS)
    summed = lax.dot_general(flat_left, flat_right, (((1,), (1,)), ((), ())), preferred_element_type=jnp.float32)
    gram = summed / jnp.float32(DOFS)
    return (filtered, gram)
```

```python
import functools

import jax
import jax.numpy as jnp
from jax import lax
from jax.experimental import pallas as pl
from jax.experimental.pallas import tpu as pltpu
from jax.sharding import PartitionSpec as P

MESH = pl.DeviceIdType.MESH
CHUNKS = 4

A = (1, 4, 1)
S = (1, -2, 1)
D = (-1, 0, 1)
TERMS = (
    (((3, S, A), (1, A, S)), ((1, A, A),), ((3, D, A),), ((3, D, D),)),
    (((3, D, A),), ((1, S, A), (1, A, S)), ((3, A, A),), ((3, A, D),)),
    (((3, D, D),), ((3, A, D),), ((1, S, A), (3, A, S)), ((1, A, A),)),
)


def lookup(table_ref, labels):
    summed = jnp.zeros(labels.shape, jnp.float32)
    for material in range(table_ref.shape[0]):
        summed = summed + jnp.where(labels == material, table_ref[material], jnp.float32(0.0))
    return summed


def kernel(
    slabs, groups, inner, unknowns,
    block, labels_ref, flags_ref, stiff_ref, dens_ref,
    out, gram_out,
    raw, planes, weights, filt, own_w, pairs, near, far,
    in_sem, hs, hr, vs, vr, out_sem, ns, nr, fs, fr,
):
    vecs, comps, ny, nz = raw.shape
    per = vecs // CHUNKS
    outer = slabs // inner
    me = lax.axis_index("slab")
    mine = lax.axis_index("vec")
    ii, oi = lax.rem(me, inner), me // inner
    near_ids = [oi * inner + lax.rem(ii + r, inner) for r in range(1, inner)]
    far_ids = [lax.rem(oi + r, outer) * inner + ii for r in range(1, outer)]
    vec_ids = [lax.rem(mine + r, groups) for r in range(1, groups)]

    loads = [
        pltpu.make_async_copy(
            block.at[pl.ds(k * per, per)], raw.at[pl.ds(k * per, per)], in_sem.at[k]
        )
        for k in range(CHUNKS)
    ]
    for copy in loads:
        copy.start()

    barrier = pltpu.get_barrier_semaphore()

    @pl.when(me > 0)
    def _():
        pl.semaphore_signal(barrier, inc=1, device_id=(me - 1, mine), device_id_type=MESH)

    @pl.when(me < slabs - 1)
    def _():
        pl.semaphore_signal(barrier, inc=1, device_id=(me + 1, mine), device_id_type=MESH)

    for peer in near_ids + far_ids:
        pl.semaphore_signal(barrier, inc=1, device_id=(peer, mine), device_id_type=MESH)
    for peer in vec_ids:
        pl.semaphore_signal(barrier, inc=1, device_id=(me, peer), device_id_type=MESH)

    labels = labels_ref[0]
    gain = jnp.sqrt(lookup(stiff_ref, labels)) * (1 - flags_ref[0]).astype(jnp.float32)
    mass = lookup(dens_ref, labels)

    for k in range(CHUNKS):
        part = pl.ds(k * per, per)
        loads[k].wait()
        planes[1, part] = (gain * raw[part].astype(jnp.float32)).astype(jnp.bfloat16)

    @pl.when(me == 0)
    def _():
        planes[0] = jnp.zeros_like(planes[0])

    @pl.when(me == slabs - 1)
    def _():
        planes[2] = jnp.zeros_like(planes[2])

    pl.semaphore_wait(
        barrier,
        len(near_ids + far_ids + vec_ids)
        + jnp.where(me > 0, 1, 0) + jnp.where(me < slabs - 1, 1, 0),
    )

    def halo(k, up):
        part = pl.ds(k * per, per)
        return pltpu.make_async_remote_copy(
            src_ref=planes.at[1, part],
            dst_ref=planes.at[0 if up else 2, part],
            send_sem=hs.at[up, k],
            recv_sem=hr.at[up, k],
            device_id=(me + 1 if up else me - 1, mine),
            device_id_type=MESH,
        )

    for k in range(CHUNKS):
        @pl.when(me < slabs - 1)
        def _():
            halo(k, 1).start()

        @pl.when(me > 0)
        def _():
            halo(k, 0).start()

    offset = (
        lax.broadcasted_iota(jnp.int32, (nz, nz), 0)
        - lax.broadcasted_iota(jnp.int32, (nz, nz), 1)
    )
    low, middle, high = offset == -1, offset == 0, offset == 1
    for source in range(3):
        for position, terms in enumerate(TERMS[source]):
            for plane in range(3):
                tap = [float(sum(f * x[plane] * y[t] for f, x, y in terms)) for t in range(3)]
                tile = jnp.where(low, tap[0], jnp.where(middle, tap[1], jnp.where(high, tap[2], 0.0)))
                weights[source, plane * nz:(plane + 1) * nz, position * nz:(position + 1) * nz] = (
                    tile.astype(jnp.bfloat16)
                )

    rows = per * ny
    row = lax.rem(lax.broadcasted_iota(jnp.int32, (rows, nz), 0), ny)
    first_row, last_row = row == 0, row == ny - 1
    factor = jnp.tile(gain * jnp.float32(-1.0 / 144.0), (per, 1))
    mass_rows = jnp.tile(mass, (per, 1))
    same = row == lax.rem(lax.broadcasted_iota(jnp.int32, (rows, rows), 1), ny)

    def flat(ref, part):
        return jnp.concatenate([ref[part, c].reshape(-1, nz) for c in range(3)], axis=-1)

    def pair(a, group, b):
        product = lax.dot_general(
            flat(own_w, pl.ds(a * per, per)),
            flat(filt.at[group], pl.ds(b * per, per)),
            (((1,), (1,)), ((), ())),
            preferred_element_type=jnp.float32,
        )
        kept = jnp.where(same, product, 0.0).reshape(per, ny, rows)
        pairs[group, a * per:(a + 1) * per, b * rows:(b + 1) * rows] = jnp.sum(kept, axis=1)

    def corner(group, k):
        for a in range(k + 1):
            pair(a, group, k)
        for b in range(k):
            pair(k, group, b)

    def share(k, r):
        part = pl.ds(k * per, per)
        return pltpu.make_async_remote_copy(
            src_ref=filt.at[mine, part],
            dst_ref=filt.at[mine, part],
            send_sem=vs.at[r - 1, k],
            recv_sem=vr.at[r - 1, k],
            device_id=(me, vec_ids[r - 1]),
            device_id_type=MESH,
        )

    def store(k):
        part = pl.ds(k * per, per)
        return pltpu.make_async_copy(filt.at[mine, part], out.at[part], out_sem.at[k])

    def others(k):
        for r in range(1, groups):
            share(k, r).wait_recv()
            corner(lax.rem(mine + groups - r, groups), k)

    for k in range(CHUNKS):
        part = pl.ds(k * per, per)

        @pl.when(me > 0)
        def _():
            halo(k, 1).wait_recv()

        @pl.when(me < slabs - 1)
        def _():
            halo(k, 0).wait_recv()

        passed = []
        for source in range(3):
            data = jnp.concatenate(
                [planes[p, part, source].reshape(rows, nz) for p in range(3)], axis=-1
            )
            passed.append(
                jnp.dot(data, weights[source], preferred_element_type=jnp.float32)
            )
        piece = lambda source, position: passed[source][:, position * nz:(position + 1) * nz]
        x = [piece(0, 0) + piece(2, 0), piece(1, 1), piece(0, 3) + piece(2, 2)]
        y = [piece(0, 1), piece(1, 2), piece(2, 3)]
        z = [piece(1, 0), piece(0, 2) + piece(2, 1), piece(1, 3)]
        for c in range(3):
            both = x[c] + y[c]
            before = jnp.where(first_row, 0.0, pltpu.roll(both - z[c], 1, 0))
            after = jnp.where(last_row, 0.0, pltpu.roll(both + z[c], rows - 1, 0))
            value = factor * (4.0 * x[c] - 2.0 * y[c] + before + after)
            value = value.astype(jnp.bfloat16)
            filt[mine, part, c] = value.reshape(per, ny, nz)
            heavy = (mass_rows * value.astype(jnp.float32)).astype(jnp.bfloat16)
            own_w[part, c] = heavy.reshape(per, ny, nz)
        for r in range(1, groups):
            share(k, r).start()
        store(k).start()
        corner(mine, k)
        if k > 0:
            others(k - 1)
    others(CHUNKS - 1)

    total_cols = groups * vecs
    fold = max(1, 128 // total_cols)
    wide = fold * total_cols
    height = vecs // fold
    gram = jnp.zeros((vecs, wide), jnp.float32)
    depth = vecs * ny
    vector = lax.broadcasted_iota(jnp.int32, (depth, wide), 0) // ny
    column = lax.rem(lax.broadcasted_iota(jnp.int32, (depth, wide), 1), total_cols)
    for group in range(groups):
        select = jnp.where(vector + group * vecs == column, 1.0, 0.0)
        gram = gram + jnp.dot(
            pairs[group], select,
            preferred_element_type=jnp.float32, precision=lax.Precision.HIGHEST,
        )
    packed = gram[:height]
    lane = lax.broadcasted_iota(jnp.int32, (height, wide), 1) // total_cols
    for f in range(1, fold):
        packed = jnp.where(lane == f, gram[f * height:(f + 1) * height], packed)

    def exchange(buffer, index, count, ids, send, recv, value):
        buffer[index] = value
        copies = [
            pltpu.make_async_remote_copy(
                src_ref=buffer.at[index],
                dst_ref=buffer.at[index],
                send_sem=send.at[r],
                recv_sem=recv.at[r],
                device_id=(ids[r], mine),
                device_id_type=MESH,
            )
            for r in range(count - 1)
        ]
        for copy in copies:
            copy.start()
        for copy in copies:
            copy.wait_recv()
        summed = buffer[0]
        for slot in range(1, count):
            summed = summed + buffer[slot]
        return summed, copies

    summed, near_copies = exchange(near, ii, inner, near_ids, ns, nr, packed)
    summed, far_copies = exchange(far, oi, outer, far_ids, fs, fr, summed)
    summed = summed / jnp.float32(unknowns)
    for f in range(fold):
        gram_out[f * height:(f + 1) * height, :] = summed[:, f * total_cols:(f + 1) * total_cols]

    for k in range(CHUNKS):
        @pl.when(me < slabs - 1)
        def _():
            halo(k, 1).wait_send()

        @pl.when(me > 0)
        def _():
            halo(k, 0).wait_send()

        for r in range(1, groups):
            share(k, r).wait_send()
        store(k).wait()
    for copy in near_copies + far_copies:
        copy.wait_send()


def shards(block, labels, flags, stiffness, density):
    slabs, groups = lax.axis_size("slab"), lax.axis_size("vec")
    vecs, comps, _, ny, nz = block.shape
    inner = 1
    while inner * inner < slabs:
        inner *= 2
    outer = slabs // inner
    total_cols = groups * vecs
    fold = max(1, 128 // total_cols)
    flat_block = block.reshape(vecs, comps, ny, nz)
    bf16, f32 = jnp.bfloat16, jnp.float32
    dma = pltpu.SemaphoreType.DMA
    vmem = pl.BlockSpec(memory_space=pltpu.VMEM)
    smem = pl.BlockSpec(memory_space=pltpu.SMEM)
    anywhere = pl.BlockSpec(memory_space=pl.ANY)
    filtered, gram = pl.pallas_call(
        functools.partial(kernel, slabs, groups, inner, comps * slabs * ny * nz),
        out_shape=(
            jax.ShapeDtypeStruct((vecs, comps, ny, nz), bf16),
            jax.ShapeDtypeStruct((vecs, total_cols), f32),
        ),
        in_specs=[anywhere, vmem, vmem, smem, smem],
        out_specs=(anywhere, vmem),
        scratch_shapes=[
            pltpu.VMEM((vecs, comps, ny, nz), bf16),
            pltpu.VMEM((3, vecs, comps, ny, nz), bf16),
            pltpu.VMEM((3, 3 * nz, 4 * nz), bf16),
            pltpu.VMEM((groups, vecs, comps, ny, nz), bf16),
            pltpu.VMEM((vecs, comps, ny, nz), bf16),
            pltpu.VMEM((groups, vecs, vecs * ny), f32),
            pltpu.VMEM((inner, vecs // fold, fold * total_cols), f32),
            pltpu.VMEM((outer, vecs // fold, fold * total_cols), f32),
            dma((CHUNKS,)),
            dma((2, CHUNKS)),
            dma((2, CHUNKS)),
            dma((groups - 1, CHUNKS)),
            dma((groups - 1, CHUNKS)),
            dma((CHUNKS,)),
            dma((inner - 1,)),
            dma((inner - 1,)),
            dma((outer - 1,)),
            dma((outer - 1,)),
        ],
        compiler_params=pltpu.CompilerParams(collective_id=0, has_side_effects=True),
        name="stiffness_gram",
    )(flat_block, labels, flags, stiffness, density)
    return filtered.reshape(block.shape), gram


def solution(mesh):
    in_specs = (
        P("vec", None, "slab", None, None),
        P("slab", None, None),
        P("slab", None, None),
        P(),
        P(),
    )
    out_specs = (P("vec", None, "slab", None, None), P("vec", None))
    return jax.shard_map(shards, mesh=mesh, in_specs=in_specs, out_specs=out_specs, check_vma=False)
```

```python
import functools

import jax
import jax.numpy as jnp
from jax import lax
from jax.experimental import pallas as pl
from jax.experimental.pallas import tpu as pltpu
from jax.sharding import PartitionSpec as P

MESH = pl.DeviceIdType.MESH
SIZES = (8, 8, 8, 4, 4)
UNIT = 8

A = (1, 4, 1)
S = (1, -2, 1)
D = (-1, 0, 1)
TERMS = (
    (((3, S, A), (1, A, S)), ((1, A, A),), ((3, D, A),), ((3, D, D),)),
    (((3, D, A),), ((1, S, A), (1, A, S)), ((3, A, A),), ((3, A, D),)),
    (((3, D, D),), ((3, A, D),), ((1, S, A), (3, A, S)), ((1, A, A),)),
)


def lookup(table_ref, labels):
    summed = jnp.zeros(labels.shape, jnp.float32)
    for material in range(table_ref.shape[0]):
        summed = summed + jnp.where(labels == material, table_ref[material], jnp.float32(0.0))
    return summed


def kernel(
    slabs, groups, inner, unknowns,
    block, labels_hbm, flags_hbm, stiff_hbm, dens_hbm,
    out, gram_out,
    raw, labels_ref, flags_ref, stiff_ref, dens_ref,
    planes, weights, shared, taken, heavy, pairs, grams, near, far,
    in_sem, hs, hr, vs, vr, ns, nr, fs, fr,
):
    vecs, comps, ny, nz = raw.shape
    cuts, part_rows = shared.shape[0], shared.shape[3]
    outer = slabs // inner
    me = lax.axis_index("slab")
    mine = lax.axis_index("vec")
    own_cut = mine if cuts > 1 else 0
    ii, oi = lax.rem(me, inner), me // inner
    vec_ids = [lax.rem(mine + r, groups) for r in range(groups)]
    near_ids = [
        (oi * inner + lax.rem(ii + r, inner), vec_ids[q])
        for q in range(cuts) for r in range(inner) if q or r
    ]
    far_ids = [(lax.rem(oi + r, outer) * inner + ii, mine) for r in range(1, outer)]
    peers = near_ids + far_ids + [(me, vec_ids[q]) for q in range(1, groups) if cuts == 1]

    barrier = pltpu.get_barrier_semaphore()

    @pl.when(me > 0)
    def _():
        pl.semaphore_signal(barrier, inc=1, device_id=(me - 1, mine), device_id_type=MESH)

    @pl.when(me < slabs - 1)
    def _():
        pl.semaphore_signal(barrier, inc=1, device_id=(me + 1, mine), device_id_type=MESH)

    for peer in peers:
        pl.semaphore_signal(barrier, inc=1, device_id=peer, device_id_type=MESH)

    tables = [
        pltpu.make_async_copy(source, target, in_sem.at[k])
        for k, (source, target) in enumerate(
            ((labels_hbm.at[0], labels_ref), (flags_hbm.at[0], flags_ref),
             (stiff_hbm, stiff_ref), (dens_hbm, dens_ref))
        )
    ]
    load = pltpu.make_async_copy(block, raw, in_sem.at[4])
    for copy in tables:
        copy.start()
    load.start()

    @pl.when(me == 0)
    def _():
        planes[0] = jnp.zeros_like(planes[0])

    @pl.when(me == slabs - 1)
    def _():
        planes[2] = jnp.zeros_like(planes[2])

    for copy in tables:
        copy.wait()
    labels = labels_ref[...]
    gain = jnp.sqrt(lookup(stiff_ref, labels)) * (1 - flags_ref[...]).astype(jnp.float32)
    mass = lookup(dens_ref, labels)
    load.wait()
    planes[1] = (gain * raw[...].astype(jnp.float32)).astype(jnp.bfloat16)

    pl.semaphore_wait(
        barrier, len(peers) + jnp.where(me > 0, 1, 0) + jnp.where(me < slabs - 1, 1, 0)
    )

    starts = [sum(SIZES[:k]) for k in range(len(SIZES))]
    parts = [pl.ds(start, size) for start, size in zip(starts, SIZES)]

    def halo(k, up):
        return pltpu.make_async_remote_copy(
            src_ref=planes.at[1, parts[k]],
            dst_ref=planes.at[0 if up else 2, parts[k]],
            send_sem=hs.at[up, k],
            recv_sem=hr.at[up, k],
            device_id=(me + 1 if up else me - 1, mine),
            device_id_type=MESH,
        )

    for k in range(len(SIZES)):
        @pl.when(me < slabs - 1)
        def _():
            halo(k, 1).start()

        @pl.when(me > 0)
        def _():
            halo(k, 0).start()

    offset = (
        lax.broadcasted_iota(jnp.int32, (nz, nz), 0)
        - lax.broadcasted_iota(jnp.int32, (nz, nz), 1)
    )
    low, middle, high = offset == -1, offset == 0, offset == 1
    for source in range(3):
        for position, terms in enumerate(TERMS[source]):
            for plane in range(3):
                tap = [float(sum(f * x[plane] * y[t] for f, x, y in terms)) for t in range(3)]
                tile = jnp.where(low, tap[0], jnp.where(middle, tap[1], jnp.where(high, tap[2], 0.0)))
                weights[source, plane * nz:(plane + 1) * nz, position * nz:(position + 1) * nz] = (
                    tile.astype(jnp.bfloat16)
                )

    scale = gain * jnp.float32(-1.0 / 144.0)
    if cuts > 1:
        own_mass = mass[:part_rows]
        for cut in range(1, cuts):
            own_mass = jnp.where(mine == cut, mass[cut * part_rows:(cut + 1) * part_rows], own_mass)
    else:
        own_mass = mass

    unit_rows = UNIT * part_rows
    same = (
        lax.rem(lax.broadcasted_iota(jnp.int32, (unit_rows, unit_rows), 0), part_rows)
        == lax.rem(lax.broadcasted_iota(jnp.int32, (unit_rows, unit_rows), 1), part_rows)
    )

    def flat(ref, unit):
        part = pl.ds(unit * UNIT, UNIT)
        return jnp.concatenate([ref[part, c].reshape(-1, nz) for c in range(3)], axis=-1)

    held = lambda r: taken.at[r - 1] if r else shared.at[own_cut]

    def pair(r, a, q, b):
        product = lax.dot_general(
            flat(heavy.at[r], a), flat(held(q), b),
            (((1,), (1,)), ((), ())),
            preferred_element_type=jnp.float32,
        )
        kept = jnp.where(same, product, 0.0).reshape(UNIT, part_rows, unit_rows)
        pairs[
            r, vec_ids[q], a * UNIT:(a + 1) * UNIT, b * unit_rows:(b + 1) * unit_rows
        ] = jnp.sum(kept, axis=1)

    done = []

    def corner(r, unit):
        done.append((r, unit))
        for q, b in done:
            if r == 0 or cuts > 1:
                pair(r, unit, q, b)
            if (q, b) != (r, unit) and (q == 0 or cuts > 1):
                pair(q, b, r, unit)

    def weigh(r, start, size):
        part = pl.ds(start, size)
        heavy[r, part] = (own_mass * held(r)[part].astype(jnp.float32)).astype(jnp.bfloat16)

    def share(k, r):
        cut = vec_ids[r] if cuts > 1 else 0
        return pltpu.make_async_remote_copy(
            src_ref=shared.at[cut, parts[k]],
            dst_ref=taken.at[groups - r - 1, parts[k]],
            send_sem=vs.at[r - 1, k],
            recv_sem=vr.at[groups - r - 1, k],
            device_id=(me, vec_ids[r]),
            device_id_type=MESH,
        )

    def arrived(k, r):
        return pltpu.make_async_remote_copy(
            src_ref=taken.at[r - 1, parts[k]],
            dst_ref=taken.at[r - 1, parts[k]],
            send_sem=vs.at[r - 1, k],
            recv_sem=vr.at[r - 1, k],
            device_id=(me, vec_ids[r]),
            device_id_type=MESH,
        )

    def others(k):
        for r in range(1, groups):
            arrived(k, r).wait_recv()
            if cuts > 1:
                weigh(r, starts[k], SIZES[k])
            if (starts[k] + SIZES[k]) % UNIT == 0:
                corner(r, starts[k] // UNIT)

    for k, size in enumerate(SIZES):
        part = parts[k]
        rows = size * ny
        row = lax.rem(lax.broadcasted_iota(jnp.int32, (rows, nz), 0), ny)
        first_row, last_row = row == 0, row == ny - 1
        factor = jnp.tile(scale, (size, 1))

        @pl.when(me > 0)
        def _():
            halo(k, 1).wait_recv()

        @pl.when(me < slabs - 1)
        def _():
            halo(k, 0).wait_recv()

        passed = []
        for source in range(3):
            data = jnp.concatenate(
                [planes[p, part, source].reshape(rows, nz) for p in range(3)], axis=-1
            )
            passed.append(
                jnp.dot(data, weights[source], preferred_element_type=jnp.float32)
            )
        piece = lambda source, position: passed[source][:, position * nz:(position + 1) * nz]
        x = [piece(0, 0) + piece(2, 0), piece(1, 1), piece(0, 3) + piece(2, 2)]
        y = [piece(0, 1), piece(1, 2), piece(2, 3)]
        z = [piece(1, 0), piece(0, 2) + piece(2, 1), piece(1, 3)]
        for c in range(3):
            both = x[c] + y[c]
            before = jnp.where(first_row, 0.0, pltpu.roll(both - z[c], 1, 0))
            after = jnp.where(last_row, 0.0, pltpu.roll(both + z[c], rows - 1, 0))
            value = factor * (4.0 * x[c] - 2.0 * y[c] + before + after)
            value = value.reshape(size, ny, nz)
            for cut in range(cuts):
                shared[cut, part, c] = (
                    value[:, cut * part_rows:(cut + 1) * part_rows].astype(jnp.bfloat16)
                )
            out[part, c] = value.astype(jnp.bfloat16)
        for r in range(1, groups):
            share(k, r).start()
        weigh(0, starts[k], size)
        if (starts[k] + size) % UNIT == 0:
            corner(0, starts[k] // UNIT)
        if k > 0:
            others(k - 1)
    others(len(SIZES) - 1)

    total_cols = groups * vecs
    fold = max(1, 128 // total_cols)
    wide = fold * total_cols
    height = vecs // fold
    depth = vecs * part_rows
    vector = lax.broadcasted_iota(jnp.int32, (depth, wide), 0) // part_rows
    column = lax.rem(lax.broadcasted_iota(jnp.int32, (depth, wide), 1), total_cols)
    lane = lax.broadcasted_iota(jnp.int32, (height, wide), 1) // total_cols
    total = jnp.zeros((cuts * vecs, wide), jnp.float32)
    for group in range(groups):
        select = jnp.where(vector + group * vecs == column, 1.0, 0.0)
        total = total + jnp.dot(
            pairs[:, group].reshape(cuts * vecs, depth), select,
            preferred_element_type=jnp.float32, precision=lax.Precision.HIGHEST,
        )
    for q in range(cuts):
        packed = total[q * vecs:q * vecs + height]
        for f in range(1, fold):
            packed = jnp.where(
                lane == f, total[q * vecs + f * height:q * vecs + (f + 1) * height], packed
            )
        grams[q] = packed

    def exchange(buffer, slot, ids, sources, send, recv):
        copies = [
            pltpu.make_async_remote_copy(
                src_ref=sources[r],
                dst_ref=buffer.at[slot],
                send_sem=send.at[r],
                recv_sem=recv.at[r],
                device_id=ids[r],
                device_id_type=MESH,
            )
            for r in range(len(ids))
        ]
        for copy in copies:
            copy.start()
        return copies

    def sum_of(buffer, copies):
        for copy in copies:
            copy.wait_recv()
        summed = buffer[0]
        for slot in range(1, buffer.shape[0]):
            summed = summed + buffer[slot]
        return summed

    near_slot = own_cut * inner + ii
    sources = [grams.at[q] for q in range(cuts) for r in range(inner) if q or r]
    near_copies = exchange(near, near_slot, near_ids, sources, ns, nr)
    near[near_slot] = grams[0]
    summed = sum_of(near, near_copies)
    far[oi] = summed
    far_copies = exchange(far, oi, far_ids, [far.at[oi]] * (outer - 1), fs, fr)
    summed = sum_of(far, far_copies) / jnp.float32(unknowns)
    for f in range(fold):
        gram_out[f * height:(f + 1) * height, :] = summed[:, f * total_cols:(f + 1) * total_cols]

    for k in range(len(SIZES)):
        @pl.when(me < slabs - 1)
        def _():
            halo(k, 1).wait_send()

        @pl.when(me > 0)
        def _():
            halo(k, 0).wait_send()

        for r in range(1, groups):
            share(k, r).wait_send()
    for copy in near_copies + far_copies:
        copy.wait_send()


def shards(block, labels, flags, stiffness, density):
    slabs, groups = lax.axis_size("slab"), lax.axis_size("vec")
    vecs, comps, _, ny, nz = block.shape
    inner = 1
    while inner * inner < slabs:
        inner *= 2
    outer = slabs // inner
    cuts = groups if ny % (8 * groups) == 0 else 1
    part_rows = ny // cuts
    total_cols = groups * vecs
    fold = max(1, 128 // total_cols)
    terms = (vecs // fold, fold * total_cols)
    flat_block = block.reshape(vecs, comps, ny, nz)
    bf16, f32, vmem = jnp.bfloat16, jnp.float32, pltpu.VMEM
    dma = pltpu.SemaphoreType.DMA
    steps = len(SIZES)
    anywhere = pl.BlockSpec(memory_space=pl.ANY)
    filtered, gram = pl.pallas_call(
        functools.partial(kernel, slabs, groups, inner, comps * slabs * ny * nz),
        out_shape=(vmem((vecs, comps, ny, nz), bf16), vmem((vecs, total_cols), f32)),
        in_specs=[anywhere] * 5,
        out_specs=(pl.BlockSpec(memory_space=vmem), pl.BlockSpec(memory_space=vmem)),
        scratch_shapes=[
            vmem((vecs, comps, ny, nz), bf16),
            vmem((ny, nz), jnp.int32),
            vmem((ny, nz), jnp.int32),
            pltpu.SMEM(stiffness.shape, f32),
            pltpu.SMEM(density.shape, f32),
            vmem((3, vecs, comps, ny, nz), bf16),
            vmem((3, 3 * nz, 4 * nz), bf16),
            vmem((cuts, vecs, comps, part_rows, nz), bf16),
            vmem((groups - 1, vecs, comps, part_rows, nz), bf16),
            vmem((cuts, vecs, comps, part_rows, nz), bf16),
            vmem((cuts, groups, vecs, vecs * part_rows), f32),
            vmem((cuts,) + terms, f32),
            vmem((cuts * inner,) + terms, f32),
            vmem((outer,) + terms, f32),
            dma((5,)),
            dma((2, steps)),
            dma((2, steps)),
            dma((groups - 1, steps)),
            dma((groups - 1, steps)),
            dma((cuts * inner - 1,)),
            dma((cuts * inner - 1,)),
            dma((outer - 1,)),
            dma((outer - 1,)),
        ],
        compiler_params=pltpu.CompilerParams(collective_id=0, has_side_effects=True),
        name="stiffness_gram",
    )(flat_block, labels, flags, stiffness, density)
    return filtered.reshape(block.shape), gram


def solution(mesh):
    in_specs = (
        P("vec", None, "slab", None, None),
        P("slab", None, None),
        P("slab", None, None),
        P(),
        P(),
    )
    out_specs = (P("vec", None, "slab", None, None), P("vec", None))
    return jax.shard_map(shards, mesh=mesh, in_specs=in_specs, out_specs=out_specs, check_vma=False)
```

```python
import functools

import jax
import jax.numpy as jnp
from jax import lax
from jax.experimental import pallas as pl
from jax.experimental.pallas import tpu as pltpu
from jax.sharding import PartitionSpec as P

MESH = pl.DeviceIdType.MESH
SIZES = (8, 16, 8)
UNIT = 8

A = (1, 4, 1)
S = (1, -2, 1)
D = (-1, 0, 1)
TERMS = (
    (((3, S, A), (1, A, S)), ((1, A, A),), ((3, D, A),), ((3, D, D),)),
    (((3, D, A),), ((1, S, A), (1, A, S)), ((3, A, A),), ((3, A, D),)),
    (((3, D, D),), ((3, A, D),), ((1, S, A), (3, A, S)), ((1, A, A),)),
)


def lookup(table_ref, labels):
    summed = jnp.zeros(labels.shape, jnp.float32)
    for material in range(table_ref.shape[0]):
        summed = summed + jnp.where(labels == material, table_ref[material], jnp.float32(0.0))
    return summed


def kernel(
    slabs, groups, inner, unknowns,
    block, labels_hbm, flags_hbm, stiff_hbm, dens_hbm,
    out, gram_out,
    raw, labels_ref, flags_ref, stiff_ref, dens_ref,
    planes, weights, shared, taken, heavy, pairs, grams, near, far,
    in_sem, hs, hr, vs, vr, ns, nr, fs, fr,
):
    vecs, comps, ny, nz = raw.shape
    cuts, part_rows = shared.shape[0], shared.shape[3]
    outer = slabs // inner
    me = lax.axis_index("slab")
    mine = lax.axis_index("vec")
    own_cut = mine if cuts > 1 else 0
    ii, oi = lax.rem(me, inner), me // inner
    vec_ids = [lax.rem(mine + r, groups) for r in range(groups)]
    near_ids = [
        (oi * inner + lax.rem(ii + r, inner), vec_ids[q])
        for q in range(cuts) for r in range(inner) if q or r
    ]
    far_ids = [(lax.rem(oi + r, outer) * inner + ii, mine) for r in range(1, outer)]
    peers = near_ids + far_ids + [(me, vec_ids[q]) for q in range(1, groups) if cuts == 1]

    barrier = pltpu.get_barrier_semaphore()

    @pl.when(me > 0)
    def _():
        pl.semaphore_signal(barrier, inc=1, device_id=(me - 1, mine), device_id_type=MESH)

    @pl.when(me < slabs - 1)
    def _():
        pl.semaphore_signal(barrier, inc=1, device_id=(me + 1, mine), device_id_type=MESH)

    for peer in peers:
        pl.semaphore_signal(barrier, inc=1, device_id=peer, device_id_type=MESH)

    tables = [
        pltpu.make_async_copy(source, target, in_sem.at[k])
        for k, (source, target) in enumerate(
            ((labels_hbm.at[0], labels_ref), (flags_hbm.at[0], flags_ref),
             (stiff_hbm, stiff_ref), (dens_hbm, dens_ref))
        )
    ]
    load = pltpu.make_async_copy(block, raw, in_sem.at[4])
    for copy in tables:
        copy.start()
    load.start()

    @pl.when(me == 0)
    def _():
        planes[0] = jnp.zeros_like(planes[0])

    @pl.when(me == slabs - 1)
    def _():
        planes[2] = jnp.zeros_like(planes[2])

    for copy in tables:
        copy.wait()
    labels = labels_ref[...]
    gain = jnp.sqrt(lookup(stiff_ref, labels)) * (1 - flags_ref[...]).astype(jnp.float32)
    mass = lookup(dens_ref, labels)
    load.wait()
    planes[1] = (gain * raw[...].astype(jnp.float32)).astype(jnp.bfloat16)

    pl.semaphore_wait(
        barrier, len(peers) + jnp.where(me > 0, 1, 0) + jnp.where(me < slabs - 1, 1, 0)
    )

    starts = [sum(SIZES[:k]) for k in range(len(SIZES))]
    parts = [pl.ds(start, size) for start, size in zip(starts, SIZES)]

    def halo(k, up):
        return pltpu.make_async_remote_copy(
            src_ref=planes.at[1, parts[k]],
            dst_ref=planes.at[0 if up else 2, parts[k]],
            send_sem=hs.at[up, k],
            recv_sem=hr.at[up, k],
            device_id=(me + 1 if up else me - 1, mine),
            device_id_type=MESH,
        )

    for k in range(len(SIZES)):
        @pl.when(me < slabs - 1)
        def _():
            halo(k, 1).start()

        @pl.when(me > 0)
        def _():
            halo(k, 0).start()

    offset = (
        lax.broadcasted_iota(jnp.int32, (nz, nz), 0)
        - lax.broadcasted_iota(jnp.int32, (nz, nz), 1)
    )
    low, middle, high = offset == -1, offset == 0, offset == 1
    for source in range(3):
        for position, terms in enumerate(TERMS[source]):
            for plane in range(3):
                tap = [float(sum(f * x[plane] * y[t] for f, x, y in terms)) for t in range(3)]
                tile = jnp.where(low, tap[0], jnp.where(middle, tap[1], jnp.where(high, tap[2], 0.0)))
                weights[source, plane * nz:(plane + 1) * nz, position * nz:(position + 1) * nz] = (
                    tile.astype(jnp.bfloat16)
                )

    scale = gain * jnp.float32(-1.0 / 144.0)
    if cuts > 1:
        own_mass = mass[:part_rows]
        for cut in range(1, cuts):
            own_mass = jnp.where(mine == cut, mass[cut * part_rows:(cut + 1) * part_rows], own_mass)
    else:
        own_mass = mass

    unit_rows = UNIT * part_rows
    same = (
        lax.rem(lax.broadcasted_iota(jnp.int32, (unit_rows, unit_rows), 0), part_rows)
        == lax.rem(lax.broadcasted_iota(jnp.int32, (unit_rows, unit_rows), 1), part_rows)
    )

    def flat(ref, unit):
        part = pl.ds(unit * UNIT, UNIT)
        return jnp.concatenate([ref[part, c].reshape(-1, nz) for c in range(3)], axis=-1)

    held = lambda r: taken.at[r - 1] if r else shared.at[own_cut]

    def pair(r, a, q, b):
        product = lax.dot_general(
            flat(heavy.at[r], a), flat(held(q), b),
            (((1,), (1,)), ((), ())),
            preferred_element_type=jnp.float32,
        )
        kept = jnp.where(same, product, 0.0).reshape(UNIT, part_rows, unit_rows)
        pairs[
            r, vec_ids[q], a * UNIT:(a + 1) * UNIT, b * unit_rows:(b + 1) * unit_rows
        ] = jnp.sum(kept, axis=1)

    done = []

    def corner(r, unit):
        done.append((r, unit))
        for q, b in done:
            if r == 0 or cuts > 1:
                pair(r, unit, q, b)
            if (q, b) != (r, unit) and (q == 0 or cuts > 1):
                pair(q, b, r, unit)

    def weigh(r, start, size):
        part = pl.ds(start, size)
        heavy[r, part] = (own_mass * held(r)[part].astype(jnp.float32)).astype(jnp.bfloat16)

    def share(k, r):
        cut = vec_ids[r] if cuts > 1 else 0
        return pltpu.make_async_remote_copy(
            src_ref=shared.at[cut, parts[k]],
            dst_ref=taken.at[groups - r - 1, parts[k]],
            send_sem=vs.at[r - 1, k],
            recv_sem=vr.at[groups - r - 1, k],
            device_id=(me, vec_ids[r]),
            device_id_type=MESH,
        )

    def arrived(k, r):
        return pltpu.make_async_remote_copy(
            src_ref=taken.at[r - 1, parts[k]],
            dst_ref=taken.at[r - 1, parts[k]],
            send_sem=vs.at[r - 1, k],
            recv_sem=vr.at[r - 1, k],
            device_id=(me, vec_ids[r]),
            device_id_type=MESH,
        )

    def others(k):
        for r in range(1, groups):
            arrived(k, r).wait_recv()
            if cuts > 1:
                weigh(r, starts[k], SIZES[k])
            for unit in range(starts[k] // UNIT, (starts[k] + SIZES[k]) // UNIT):
                corner(r, unit)

    for k, size in enumerate(SIZES):
        part = parts[k]
        rows = size * ny
        row = lax.rem(lax.broadcasted_iota(jnp.int32, (rows, nz), 0), ny)
        first_row, last_row = row == 0, row == ny - 1
        factor = jnp.tile(scale, (size, 1))

        @pl.when(me > 0)
        def _():
            halo(k, 1).wait_recv()

        @pl.when(me < slabs - 1)
        def _():
            halo(k, 0).wait_recv()

        passed = []
        for source in range(3):
            data = jnp.concatenate(
                [planes[p, part, source].reshape(rows, nz) for p in range(3)], axis=-1
            )
            passed.append(
                jnp.dot(data, weights[source], preferred_element_type=jnp.float32)
            )
        piece = lambda source, position: passed[source][:, position * nz:(position + 1) * nz]
        x = [piece(0, 0) + piece(2, 0), piece(1, 1), piece(0, 3) + piece(2, 2)]
        y = [piece(0, 1), piece(1, 2), piece(2, 3)]
        z = [piece(1, 0), piece(0, 2) + piece(2, 1), piece(1, 3)]
        for c in range(3):
            both = x[c] + y[c]
            before = jnp.where(first_row, 0.0, pltpu.roll(both - z[c], 1, 0))
            after = jnp.where(last_row, 0.0, pltpu.roll(both + z[c], rows - 1, 0))
            value = factor * (4.0 * x[c] - 2.0 * y[c] + before + after)
            value = value.reshape(size, ny, nz)
            for cut in range(cuts):
                shared[cut, part, c] = (
                    value[:, cut * part_rows:(cut + 1) * part_rows].astype(jnp.bfloat16)
                )
            out[part, c] = value.astype(jnp.bfloat16)
        for r in range(1, groups):
            share(k, r).start()
        weigh(0, starts[k], size)
        for unit in range(starts[k] // UNIT, (starts[k] + size) // UNIT):
            corner(0, unit)
        if k > 0:
            others(k - 1)
    others(len(SIZES) - 1)

    total_cols = groups * vecs
    fold = max(1, 128 // total_cols)
    wide = fold * total_cols
    height = vecs // fold
    depth = vecs * part_rows
    vector = lax.broadcasted_iota(jnp.int32, (depth, wide), 0) // part_rows
    column = lax.rem(lax.broadcasted_iota(jnp.int32, (depth, wide), 1), total_cols)
    lane = lax.broadcasted_iota(jnp.int32, (height, wide), 1) // total_cols
    total = jnp.zeros((cuts * vecs, wide), jnp.float32)
    for group in range(groups):
        select = jnp.where(vector + group * vecs == column, 1.0, 0.0)
        total = total + jnp.dot(
            pairs[:, group].reshape(cuts * vecs, depth), select,
            preferred_element_type=jnp.float32, precision=lax.Precision.HIGHEST,
        )
    for q in range(cuts):
        packed = total[q * vecs:q * vecs + height]
        for f in range(1, fold):
            packed = jnp.where(
                lane == f, total[q * vecs + f * height:q * vecs + (f + 1) * height], packed
            )
        grams[q] = packed

    def exchange(buffer, slot, ids, sources, send, recv):
        copies = [
            pltpu.make_async_remote_copy(
                src_ref=sources[r],
                dst_ref=buffer.at[slot],
                send_sem=send.at[r],
                recv_sem=recv.at[r],
                device_id=ids[r],
                device_id_type=MESH,
            )
            for r in range(len(ids))
        ]
        for copy in copies:
            copy.start()
        return copies

    def sum_of(buffer, copies):
        for copy in copies:
            copy.wait_recv()
        summed = buffer[0]
        for slot in range(1, buffer.shape[0]):
            summed = summed + buffer[slot]
        return summed

    near_slot = own_cut * inner + ii
    sources = [grams.at[q] for q in range(cuts) for r in range(inner) if q or r]
    near_copies = exchange(near, near_slot, near_ids, sources, ns, nr)
    near[near_slot] = grams[0]
    summed = sum_of(near, near_copies)
    far[oi] = summed
    far_copies = exchange(far, oi, far_ids, [far.at[oi]] * (outer - 1), fs, fr)
    summed = sum_of(far, far_copies) / jnp.float32(unknowns)
    for f in range(fold):
        gram_out[f * height:(f + 1) * height, :] = summed[:, f * total_cols:(f + 1) * total_cols]

    for k in range(len(SIZES)):
        @pl.when(me < slabs - 1)
        def _():
            halo(k, 1).wait_send()

        @pl.when(me > 0)
        def _():
            halo(k, 0).wait_send()

        for r in range(1, groups):
            share(k, r).wait_send()
    for copy in near_copies + far_copies:
        copy.wait_send()


def shards(block, labels, flags, stiffness, density):
    slabs, groups = lax.axis_size("slab"), lax.axis_size("vec")
    vecs, comps, _, ny, nz = block.shape
    inner = 1
    while inner * inner < slabs:
        inner *= 2
    outer = slabs // inner
    cuts = groups if ny % (8 * groups) == 0 else 1
    part_rows = ny // cuts
    total_cols = groups * vecs
    fold = max(1, 128 // total_cols)
    terms = (vecs // fold, fold * total_cols)
    flat_block = block.reshape(vecs, comps, ny, nz)
    bf16, f32, vmem = jnp.bfloat16, jnp.float32, pltpu.VMEM
    dma = pltpu.SemaphoreType.DMA
    steps = len(SIZES)
    anywhere = pl.BlockSpec(memory_space=pl.ANY)
    filtered, gram = pl.pallas_call(
        functools.partial(kernel, slabs, groups, inner, comps * slabs * ny * nz),
        out_shape=(vmem((vecs, comps, ny, nz), bf16), vmem((vecs, total_cols), f32)),
        in_specs=[anywhere] * 5,
        out_specs=(pl.BlockSpec(memory_space=vmem), pl.BlockSpec(memory_space=vmem)),
        scratch_shapes=[
            vmem((vecs, comps, ny, nz), bf16),
            vmem((ny, nz), jnp.int32),
            vmem((ny, nz), jnp.int32),
            pltpu.SMEM(stiffness.shape, f32),
            pltpu.SMEM(density.shape, f32),
            vmem((3, vecs, comps, ny, nz), bf16),
            vmem((3, 3 * nz, 4 * nz), bf16),
            vmem((cuts, vecs, comps, part_rows, nz), bf16),
            vmem((groups - 1, vecs, comps, part_rows, nz), bf16),
            vmem((cuts, vecs, comps, part_rows, nz), bf16),
            vmem((cuts, groups, vecs, vecs * part_rows), f32),
            vmem((cuts,) + terms, f32),
            vmem((cuts * inner,) + terms, f32),
            vmem((outer,) + terms, f32),
            dma((5,)),
            dma((2, steps)),
            dma((2, steps)),
            dma((groups - 1, steps)),
            dma((groups - 1, steps)),
            dma((cuts * inner - 1,)),
            dma((cuts * inner - 1,)),
            dma((outer - 1,)),
            dma((outer - 1,)),
        ],
        compiler_params=pltpu.CompilerParams(collective_id=0, has_side_effects=True),
        name="stiffness_gram",
    )(flat_block, labels, flags, stiffness, density)
    return filtered.reshape(block.shape), gram


def solution(mesh):
    in_specs = (
        P("vec", None, "slab", None, None),
        P("slab", None, None),
        P("slab", None, None),
        P(),
        P(),
    )
    out_specs = (P("vec", None, "slab", None, None), P("vec", None))
    return jax.shard_map(shards, mesh=mesh, in_specs=in_specs, out_specs=out_specs, check_vma=False)
```
